32 devices in a mesh: ctx: 8 (over z, x), head: 4 (over y, core).
Axes of the slice: x: 2, y: 2, z: 4, core: 2. Of those that a mesh axis runs over, the one named last changes fastest.
Arguments:
- queries: bfloat16 [1024, 4096], P('ctx', 'head'), may hold values from -24 to 24
- key_rows: bfloat16 [1024, 4096], P('ctx', 'head'), may hold values from -24 to 24
- value_rows: bfloat16 [1024, 4096], P('ctx', 'head'), may hold values from -6 to 6
- upstream: bfloat16 [1024, 6144], P('ctx', 'head'), may hold values from -6 to 6
- out_weight: bfloat16 [6144, 4096], P('ctx', 'head'), may hold values from -0.078125 to 0.078125
- group_ids: int32 [1024], replicated, may hold values from 0 to 7, never falling along the last dimension, each value on 1 to 256 neighbouring positions
Outputs:
- grad_queries: bfloat16 [1024, 4096], P('ctx', 'head')
- grad_keys: bfloat16 [1024, 4096], P('ctx', 'head')
- grad_values: bfloat16 [1024, 4096], P('ctx', 'head')
The draws below stay inside these ranges and needn't reach their ends.
Inputs may be any that keep to these rules, and one draw needn't show every extreme that they name: `group_ids`: never falling along the tokens; each group number covers 1 to 256 consecutive tokens, one exactly 256.
All inputs are finite; a program needn't handle non-finite values.
Results may differ from the reference program's by a relative error of at most 0.025.
Values may be sent and summed in bfloat16 or wider, within the bound.
No kernel may reach another device: no remote copies, remote signals or barrier semaphores. Data moves between devices by JAX's collectives and lax.ppermute only.
A program may use at most 64 MiB of HBM per device.

```python
import math
import jax
import jax.numpy as jnp
import numpy as np
from jax import lax

D = 6144
HEADS = 32
HDIM = 128
GROUP = 128
TOKENS = 1024


def drawn_pair(key):
    full_width = HEADS * HDIM
    query_base = jnp.clip(jax.random.normal(jax.random.fold_in(key, 101), (TOKENS, full_width), jnp.float32), -6.0, 6.0)
    key_base = jnp.clip(jax.random.normal(jax.random.fold_in(key, 102), (TOKENS, full_width), jnp.float32), -6.0, 6.0)
    return (query_base, key_base)


def draw_queries(key, part):
    return drawn_pair(key)[0].astype(jnp.bfloat16)


def draw_key_rows(key, part):
    return drawn_pair(key)[1].astype(jnp.bfloat16)


def block_levels(own_key, dims, shards, low, high):
    def one(dim, shards_of):
        heights = jax.random.uniform(jax.random.fold_in(jax.random.fold_in(own_key, 6), dim), (shards_of,), jnp.float32, low / len(shards), high / len(shards))
        return jnp.repeat(jnp.exp(heights), dims[dim] // shards_of).reshape((-1,) + (1,) * (len(dims) - dim - 1))

    factor_of = one(*shards[0])
    for cut in shards[1:]:
        factor_of = factor_of * one(*cut)
    return factor_of


def length_profile(count, total, limit, slope):
    portions = [(1 << 20) // math.isqrt(standing ** slope) + 1 for standing in range(2, count + 1)]
    surplus, given = total - limit - (count - 1), [1] * (count - 1)
    while surplus > 0:
        movable = [i for i in range(count - 1) if given[i] < limit]
        whole, left = sum([portions[i] for i in movable]), surplus
        for i in movable:
            more = min(limit - given[i], max(1, left * portions[i] // whole), surplus)
            given[i] = given[i] + more
            surplus = surplus - more
    return np.array([limit] + given)


def ragged(stream_key, count, total, bound, slope):
    if count == 2:
        one = jax.random.randint(stream_key, (), max(1, total - bound), min(bound, total - 1) + 1)
        return jnp.stack([one, total - one])
    tallies = jnp.asarray(length_profile(count, total, bound, slope), jnp.int32)
    pairs = (count - 1) // 2
    giver, taker = tallies[1:1 + 2 * pairs:2], tallies[2:2 + 2 * pairs:2]
    room = jnp.minimum(giver - 1, bound - taker)
    passed = jax.random.randint(jax.random.fold_in(stream_key, 1), (pairs,), 0, 1 << 20) % (room + 1)
    tallies = tallies.at[1:1 + 2 * pairs:2].set(giver - passed).at[2:2 + 2 * pairs:2].set(taker + passed)
    return tallies[jax.random.permutation(jax.random.fold_in(stream_key, 2), count)]


def scatter_about(rng, extent, scale, most, split=(), kind=jnp.bfloat16):
    drawn = scale * jax.random.normal(rng, extent, jnp.float32)
    if split:
        drawn = drawn * block_levels(rng, extent, split, -0.22, 0.18)
    return jnp.clip(drawn, -most, most).astype(kind)


def setup_inputs(seed: int = 0) -> dict:
    key_of = jax.random.split(jax.random.key(seed), 7)
    queries = draw_queries(jax.random.fold_in(key_of[6], 71), 0)
    key_rows = draw_key_rows(jax.random.fold_in(key_of[6], 71), 0)
    value_rows = scatter_about(key_of[2], (TOKENS, HEADS * HDIM), 1.0, 6.0, ((0, 8), (1, 4)))
    upstream = scatter_about(key_of[3], (TOKENS, D), 1.0, 6.0, ((0, 8), (1, 4)))
    out_weight = scatter_about(key_of[4], (D, HEADS * HDIM), D ** -0.5, 0.078125, ((0, 8), (1, 4)))
    group_ids = jnp.searchsorted(jnp.cumsum(ragged(key_of[5], TOKENS // GROUP, TOKENS, 2 * GROUP, 1)), jnp.arange(TOKENS), side="right").astype(jnp.int32)
    return dict(queries=queries, key_rows=key_rows, value_rows=value_rows, upstream=upstream, out_weight=out_weight, group_ids=group_ids)


def reference(queries, key_rows, value_rows, upstream, out_weight, group_ids):
    scaling = HDIM ** -0.5
    grad_out = jnp.dot(upstream, out_weight, preferred_element_type=jnp.float32).astype(jnp.bfloat16)
    total_rows = queries.shape[0]
    heads_all = queries.shape[1] // HDIM
    allowed = group_ids[None, :] <= group_ids[:, None]

    def heads_first(matrix):
        return matrix.reshape(total_rows, heads_all, HDIM).transpose(1, 0, 2)

    def one_head(operands):
        query_head, key_head, value_head, grad_head = operands
        scores = scaling * jnp.dot(query_head, key_head.T, preferred_element_type=jnp.float32)
        row_max = jnp.max(jnp.where(allowed, scores, -1.0e30), axis=1)
        weights = jnp.where(allowed, jnp.exp(scores - row_max[:, None]), 0.0)
        log_total = row_max + jnp.log(jnp.sum(weights, axis=1))
        probs = jnp.where(allowed, jnp.exp(scores - log_total[:, None]), 0.0)
        probs_low = probs.astype(jnp.bfloat16)
        attn_out = jnp.dot(probs_low, value_head, preferred_element_type=jnp.float32)
        delta = jnp.sum(grad_head.astype(jnp.float32) * attn_out, axis=1)
        grad_probs = jnp.dot(grad_head, value_head.T, preferred_element_type=jnp.float32)
        mixed = (probs * grad_probs).astype(jnp.bfloat16)
        grad_query = scaling * (jnp.dot(mixed, key_head, preferred_element_type=jnp.float32)
                                - delta[:, None] * jnp.dot(probs_low, key_head, preferred_element_type=jnp.float32))
        grad_scores = (probs * (grad_probs - delta[:, None])).astype(jnp.bfloat16)
        grad_key = scaling * jnp.dot(grad_scores.T, query_head, preferred_element_type=jnp.float32)
        grad_value = jnp.dot(probs_low.T, grad_head, preferred_element_type=jnp.float32)
        return (grad_query, grad_key, grad_value)

    results = lax.map(one_head, (heads_first(queries), heads_first(key_rows), heads_first(value_rows), heads_first(grad_out)))

    def tokens_first(stacked):
        return stacked.transpose(1, 0, 2).reshape(total_rows, heads_all * HDIM).astype(jnp.bfloat16)

    return (tokens_first(results[0]), tokens_first(results[1]), tokens_first(results[2]))
```

```python
import math

import jax
import jax.numpy as jnp
from jax import lax
from jax.experimental import pallas as pl
from jax.experimental.pallas import tpu as pltpu
from jax.sharding import PartitionSpec as P

HDIM = 128
MAX_GROUP = 256


masked_score = -1e30
VM = pltpu.VMEM
F32 = jnp.float32
BF16 = jnp.bfloat16


def general_body(queries, key_rows, value_rows, upstream, out_weight, group_ids):
    rows_dev = queries.shape[0]
    heads_dev = queries.shape[1] // HDIM
    scaling = HDIM ** (-0.5)
    own_start = lax.axis_index("ctx") * rows_dev
    own_ids = lax.dynamic_slice_in_dim(group_ids, own_start, rows_dev, 0)
    upstream_full = lax.all_gather(upstream, "head", axis=1, tiled=True)
    grad_out = jnp.dot(
        upstream_full,
        lax.all_gather(out_weight, "ctx", axis=0, tiled=True),
        preferred_element_type=jnp.float32,
    ).astype(jnp.bfloat16)
    query_heads = queries.reshape(rows_dev, heads_dev, HDIM)
    grad_heads = grad_out.reshape(rows_dev, heads_dev, HDIM)
    key_heads = key_rows.reshape(rows_dev, heads_dev, HDIM)
    value_heads = value_rows.reshape(rows_dev, heads_dev, HDIM)
    key_piece = lax.all_gather(key_rows, "ctx", axis=0, tiled=True)
    value_piece = lax.all_gather(value_rows, "ctx", axis=0, tiled=True)
    key_block = key_piece.reshape(-1, heads_dev, HDIM)
    value_block = value_piece.reshape(-1, heads_dev, HDIM)
    allowed = (group_ids[None, :] <= own_ids[:, None])[None]
    scores = scaling * jnp.einsum(
        "qhd,khd->hqk", query_heads, key_block, preferred_element_type=jnp.float32
    )
    scores = jnp.where(allowed, scores, masked_score)
    run_max = jnp.max(scores, axis=2)
    weights = jnp.where(allowed, jnp.exp(scores - run_max[:, :, None]), 0.0)
    log_total = run_max + jnp.log(jnp.sum(weights, axis=2))
    probs = jnp.where(allowed, jnp.exp(scores - log_total[:, :, None]), 0.0)
    probs_low = probs.astype(jnp.bfloat16)
    grad_probs = jnp.einsum(
        "qhd,khd->hqk", grad_heads, value_block, preferred_element_type=jnp.float32
    )
    mixed_low = (probs * grad_probs).astype(jnp.bfloat16)
    attn_out = jnp.einsum(
        "hqk,khd->hqd", probs_low, value_block, preferred_element_type=jnp.float32
    )
    mixed_acc = jnp.einsum(
        "hqk,khd->hqd", mixed_low, key_block, preferred_element_type=jnp.float32
    )
    plain_acc = jnp.einsum(
        "hqk,khd->hqd", probs_low, key_block, preferred_element_type=jnp.float32
    )
    delta = jnp.einsum("qhd,hqd->hq", grad_heads.astype(jnp.float32), attn_out)
    grad_query = scaling * (mixed_acc - delta[:, :, None] * plain_acc)
    grad_queries = (
        grad_query.transpose(1, 0, 2).reshape(rows_dev, heads_dev * HDIM).astype(jnp.bfloat16)
    )
    piece_lse = lax.all_gather(log_total.T, "ctx", axis=0, tiled=True).T
    piece_delta = lax.all_gather(delta.T, "ctx", axis=0, tiled=True).T
    query_block = lax.all_gather(queries, "ctx", axis=0, tiled=True).reshape(-1, heads_dev, HDIM)
    grad_block = lax.all_gather(grad_out, "ctx", axis=0, tiled=True).reshape(-1, heads_dev, HDIM)
    allowed = (own_ids[None, :] <= group_ids[:, None])[None]
    scores = scaling * jnp.einsum(
        "qhd,khd->hqk", query_block, key_heads, preferred_element_type=jnp.float32
    )
    probs = jnp.where(allowed, jnp.exp(scores - piece_lse[:, :, None]), 0.0)
    probs_low = probs.astype(jnp.bfloat16)
    grad_probs = jnp.einsum(
        "qhd,khd->hqk", grad_block, value_heads, preferred_element_type=jnp.float32
    )
    grad_scores = (probs * (grad_probs - piece_delta[:, :, None])).astype(jnp.bfloat16)
    value_grad = jnp.einsum(
        "hqk,qhd->hkd", probs_low, grad_block, preferred_element_type=jnp.float32
    )
    key_grad = jnp.einsum(
        "hqk,qhd->hkd", grad_scores, query_block, preferred_element_type=jnp.float32
    )
    grad_keys = (
        (scaling * key_grad)
        .transpose(1, 0, 2)
        .reshape(rows_dev, heads_dev * HDIM)
        .astype(jnp.bfloat16)
    )
    grad_values = (
        value_grad.transpose(1, 0, 2).reshape(rows_dev, heads_dev * HDIM).astype(jnp.bfloat16)
    )
    return (grad_queries, grad_keys, grad_values)


CHUNKS = ((0, 4), (2, 6), (1, 5), (3, 7))


def call(kernel, out_shape, n_in, n_scalar, scratch=(), flops=0, nbytes=0):
    spec = pl.BlockSpec(memory_space=VM)
    return pl.pallas_call(
        kernel,
        out_shape=out_shape,
        in_specs=[pl.BlockSpec(memory_space=pltpu.SMEM)] * n_scalar + [spec] * n_in,
        out_specs=jax.tree.map(lambda _: spec, out_shape),
        scratch_shapes=list(scratch),
        cost_estimate=pl.CostEstimate(flops=flops, bytes_accessed=nbytes, transcendentals=0),
    )


def head_of(c, n_z):
    return (c % 2) * n_z + c // 2


def pack_kernel(n, n_z, c_ref, q_ref, k_ref, v_ref, *out_refs):
    c = c_ref[0]
    for d in range(n):
        col = pl.multiple_of(head_of(c ^ d, n_z) * HDIM, HDIM)
        for i, ref in enumerate((q_ref, k_ref, v_ref)):
            out_refs[d][i] = ref[:, pl.ds(col, HDIM)]


def unpack_kernel(n, n_z, c_ref, *refs):
    c = c_ref[0]
    for d in range(n):
        col = pl.multiple_of(head_of(c ^ d, n_z) * HDIM, HDIM)
        for i, ref in enumerate(refs[n:]):
            ref[:, pl.ds(col, HDIM)] = refs[d][i]


def matmul_kernel(n_up, n_z, c_ref, *refs):
    up_refs, (own_ref, got_ref), out_refs, acc_ref = (
        refs[:n_up], refs[n_up:n_up + 2], refs[n_up + 2:-1], refs[-1],
    )
    c = c_ref[0]
    x, z = c % 2, c // 2
    depth, half = got_ref.shape
    rows = up_refs[0].shape[0]
    own_k = pl.multiple_of(x * depth, HDIM)
    got_k = pl.multiple_of((1 - x) * depth, HDIM)
    cols = pl.multiple_of(x * half, HDIM)
    for m in range(n_up):
        acc_ref[m * rows:(m + 1) * rows, :] = jnp.dot(
            up_refs[m][:, pl.ds(own_k, depth)], own_ref[:, pl.ds(cols, half)],
            preferred_element_type=F32,
        ) + jnp.dot(
            up_refs[m][:, pl.ds(got_k, depth)], got_ref[...], preferred_element_type=F32
        )
    for d in range(n_z):
        col = pl.multiple_of((z ^ d) * HDIM, HDIM)
        out_refs[d][...] = acc_ref[:, pl.ds(col, HDIM)].astype(out_refs[d].dtype)


def key_limit(b, block, tokens):
    limit = (b + 1) * block + MAX_GROUP - 1
    return min(tokens, -(-limit // block) * block)


def probs_kernel(n, block, c_ref, end_ref, *refs):
    piece_refs, (pt_ref, q_ref, k_ref, v_ref) = refs[:n], refs[n:]
    c = c_ref[0]
    rows = piece_refs[0].shape[1]
    tokens = q_ref.shape[0]
    for d in range(n):
        at = pl.ds(pl.multiple_of((c ^ d) * rows, rows), rows)
        for i, ref in enumerate((q_ref, k_ref, v_ref)):
            ref[at, :] = piece_refs[d][i]
    factor = HDIM ** (-0.5) * math.log2(math.e)
    for b in range(tokens // block):
        first, limit = b * block, key_limit(b, block, tokens)
        cols = slice(first, first + block)
        s = factor * lax.dot_general(
            k_ref[:limit, :], q_ref[cols, :], (((1,), (1,)), ((), ())),
            preferred_element_type=F32,
        )
        key = first + lax.broadcasted_iota(jnp.int32, (limit - first, block), 0)
        near = jnp.where(key < end_ref[:, cols], s[first:, :], masked_score)
        top = jnp.max(near, axis=0, keepdims=True)
        if first:
            top = jnp.maximum(top, jnp.max(s[:first, :], axis=0, keepdims=True))
        e_near = jnp.exp2(near - top)
        total = jnp.sum(e_near, axis=0, keepdims=True)
        if first:
            e_far = jnp.exp2(s[:first, :] - top)
            total = total + jnp.sum(e_far, axis=0, keepdims=True)
        inverse = 1.0 / total
        pt_ref[first:limit, cols] = (e_near * inverse).astype(BF16)
        if first:
            pt_ref[:first, cols] = (e_far * inverse).astype(BF16)


def grads_kernel(n, n_z, block, chunks, c_ref, t_ref, pt_ref, q_ref, k_ref, v_ref, *refs):
    n_do = n_z * len(chunks)
    do_refs, out_refs = refs[:n_do], refs[n_do:n_do + n]
    do_s, kt_s, dq_s, dk_s, dv_s = refs[n_do + n:]
    c, t = c_ref[0], t_ref[0]
    tokens = q_ref.shape[0]
    rows = tokens // n
    for i, blocks in enumerate(chunks):
        total = do_refs[i * n_z][...].astype(F32)
        for d in range(1, n_z):
            total = total + do_refs[i * n_z + d][...].astype(F32)
        total = total.astype(BF16)
        for j, m in enumerate(blocks):
            at = pl.ds(pl.multiple_of((t ^ m) * rows, rows), rows)
            do_s[at, :] = total[j * rows:(j + 1) * rows, :]
    kt_s[...] = k_ref[...].T
    scaling = HDIM ** (-0.5)
    n_blocks = tokens // block
    seen = 0
    for b in range(n_blocks):
        first, limit = b * block, key_limit(b, block, tokens)
        cols = slice(first, first + block)
        do = do_s[cols, :]
        p_low = pt_ref[:limit, cols]
        dp = lax.dot_general(
            v_ref[:limit, :], do, (((1,), (1,)), ((), ())), preferred_element_type=F32
        )
        p = p_low.astype(F32)
        delta = jnp.sum(p * dp, axis=0, keepdims=True)
        ds = (p * (dp - delta)).astype(BF16)
        dv = jnp.dot(p_low, do, preferred_element_type=F32)
        dk = jnp.dot(ds, q_ref[cols, :], preferred_element_type=F32)
        dq = jnp.dot(kt_s[:, :limit], ds, preferred_element_type=F32)
        dq_s[cols, :] = (scaling * dq.T).astype(BF16)
        if seen:
            dv_s[:seen, :] += dv[:seen, :]
            dk_s[:seen, :] += dk[:seen, :]
        if limit > seen:
            dv_s[seen:limit, :] = dv[seen:, :]
            dk_s[seen:limit, :] = dk[seen:, :]
        seen = limit
    for d in range(n):
        at = pl.ds(pl.multiple_of((c ^ d) * rows, rows), rows)
        out_refs[d][0] = dq_s[at, :]
        out_refs[d][1] = (scaling * dk_s[at, :]).astype(BF16)
        out_refs[d][2] = dv_s[at, :].astype(BF16)


def spread_body(n, n_head, queries, key_rows, value_rows, upstream, out_weight, group_ids):
    n_z = n // 2
    rows = queries.shape[0]
    tokens = n * rows
    axes = ("ctx", "head")
    block = max(MAX_GROUP, rows)

    def perm(move):
        pairs = []
        for c in range(n):
            for h in range(n_head):
                z, x, y, k = move(c // 2, c % 2, h // 2, h % 2)
                pairs.append((c * n_head + h, (z * 2 + x) * n_head + y * 2 + k))
        return pairs

    def send(value, move):
        return lax.ppermute(value, axes, perm(move))

    def swap_x(value):
        return send(value, lambda z, x, y, k: (z, 1 - x, y, k))

    def swap_y(value):
        return send(value, lambda z, x, y, k: (z, x, 1 - y, k))

    def swap_k(value):
        return send(value, lambda z, x, y, k: (z, x, y, 1 - k))

    c = lax.axis_index("ctx")
    h = lax.axis_index("head")
    c1 = c.reshape(1).astype(jnp.int32)
    x, y, k = c % 2, h // 2, h % 2
    t1 = (x + 2 * y + 4 * k).reshape(1).astype(jnp.int32)

    half = out_weight.shape[1] // 2
    w_send = lax.dynamic_slice_in_dim(out_weight, (1 - x) * half, half, 1)
    w_got = swap_x(w_send)
    up = {0: send(upstream, lambda z, x, y, k: (y * 2 + k, x, z % 2, z // 2))}
    up[1] = swap_x(up[0])
    up[2] = swap_y(up[0])
    up[4] = swap_k(up[0])
    up[6] = swap_k(up[2])
    up[5] = swap_k(up[1])
    up[3] = swap_y(up[1])
    up[7] = swap_k(up[3])

    end = jnp.sum(group_ids[None, :] <= group_ids[:, None], axis=1, dtype=jnp.int32)[None]
    piece = jax.ShapeDtypeStruct((3, rows, HDIM), BF16)
    pieces = call(
        lambda *r: pack_kernel(n, n_z, *r), [piece] * n, 3, 1, nbytes=6 * rows * n * HDIM * 2
    )(c1, queries, key_rows, value_rows)
    got = [pieces[0]] + [
        lax.ppermute(pieces[d], "ctx", [(i, i ^ d) for i in range(n)]) for d in range(1, n)
    ]
    head = jax.ShapeDtypeStruct((tokens, HDIM), BF16)
    pt, q, kk, v = call(
        lambda *r: probs_kernel(n, block, *r),
        [jax.ShapeDtypeStruct((tokens, tokens), BF16), head, head, head], n + 1, 1,
        flops=2 * tokens * tokens * HDIM, nbytes=4 * tokens * tokens,
    )(c1, end, *got)

    grads = []
    for blocks in CHUNKS:
        size = len(blocks) * rows
        part = [jax.ShapeDtypeStruct((size, HDIM), F32 if d == 0 else BF16) for d in range(n_z)]
        parts = call(
            lambda *r: matmul_kernel(len(blocks), n_z, *r), part, len(blocks) + 2, 1,
            scratch=[VM((size, half), F32)],
            flops=2 * size * half * upstream.shape[1], nbytes=half * upstream.shape[1] * 2,
        )(c1, *[up[m] for m in blocks], out_weight, w_got)
        grads.append(parts[0])
        for d in range(1, n_z):
            grads.append(send(parts[d], lambda z, x, y, k, d=d: (z ^ d, x, y, k)))

    outs = call(
        lambda *r: grads_kernel(n, n_z, block, CHUNKS, *r), [piece] * n, 4 + len(grads), 2,
        scratch=[VM((tokens, HDIM), BF16), VM((HDIM, tokens), BF16), VM((tokens, HDIM), BF16),
                 VM((tokens, HDIM), F32), VM((tokens, HDIM), F32)],
        flops=8 * tokens * tokens * HDIM, nbytes=4 * tokens * tokens,
    )(c1, t1, pt, q, kk, v, *grads)
    back = [outs[0]] + [
        lax.ppermute(outs[d], "ctx", [(i, i ^ d) for i in range(n)]) for d in range(1, n)
    ]
    full = jax.ShapeDtypeStruct((rows, n * HDIM), BF16)
    return tuple(call(
        lambda *r: unpack_kernel(n, n_z, *r), [full] * 3, n, 1, nbytes=6 * rows * n * HDIM * 2
    )(c1, *back))


def solution(mesh):
    n, n_head = mesh.shape["ctx"], mesh.shape["head"]

    def body(*args):
        heads_dev = args[0].shape[1] // HDIM
        rows, tokens = args[0].shape[0], args[5].shape[0]
        if n == 8 and n_head == 4 and heads_dev == n and tokens % max(MAX_GROUP, rows) == 0:
            return spread_body(n, n_head, *args)
        return general_body(*args)

    in_specs = (
        P("ctx", "head"),
        P("ctx", "head"),
        P("ctx", "head"),
        P("ctx", "head"),
        P("ctx", "head"),
        P(),
    )
    out_specs = (P("ctx", "head"), P("ctx", "head"), P("ctx", "head"))
    return jax.shard_map(body, mesh=mesh, in_specs=in_specs, out_specs=out_specs, check_vma=False)
```
